128 devices in a mesh: seq: 128 (over x, z, y, core).
Axes of the slice: x: 4, y: 4, z: 4, core: 2. Of those that a mesh axis runs over, the one named last changes fastest.
Arguments:
- activations: bfloat16 [262144, 384], P('seq'), may hold values from -6 to 6
- conv_weight: bfloat16 [4, 3, 384, 384], replicated, may hold values from -0.1875 to 0.1875
- conv_bias: float32 [4, 384], replicated, may hold values from -3 to 3
- conv_gain: float32 [4, 384], replicated, may hold values from 0.1 to 1.9
- mlp_gain: float32 [4, 384], replicated, may hold values from 0.1 to 1.9
- w_in: bfloat16 [4, 384, 768], replicated, may hold values from -0.3125 to 0.3125
- w_out: bfloat16 [4, 768, 384], replicated, may hold values from -0.21875 to 0.21875
Outputs:
- channel_major: bfloat16 [384, 262144], P('seq')
The draws below stay inside these ranges and needn't reach their ends.
All inputs are finite; a program needn't handle non-finite values.
Results may differ from the reference program's by a relative error of at most 0.015.
Values may be sent and summed in bfloat16 or wider, within the bound.
A program may use at most 64 MiB of HBM per device.

```python
import jax
import jax.numpy as jnp
from jax import lax

C = 384
HID = 768
LAYERS = 4
S_DEV = 2048
LENGTH = 262144


def steps_of(own_key, extent, cuts, low, largest):
    level, own = 1.0, jax.random.fold_in(own_key, 6)
    for axis_at, shards_of in cuts:
        heights = jnp.exp(jax.random.uniform(jax.random.fold_in(own, axis_at), (shards_of,), jnp.float32, low / len(cuts), largest / len(cuts)))
        level = level * jnp.repeat(heights, extent[axis_at] // shards_of).reshape([-1 if axis == axis_at else 1 for axis in range(len(extent))])
    return level


def gaussian(key, dims, width, limit, cuts=(), dtype=jnp.bfloat16):
    factor_of = steps_of(key, dims, cuts, -0.22, 0.18) if cuts else 1.0
    entries = jax.random.normal(key, dims, jnp.float32) * width * factor_of
    return jnp.minimum(jnp.maximum(entries, -limit), limit).astype(dtype)


def setup_inputs(seed: int = 0) -> dict:
    key_of = jax.random.split(jax.random.key(seed), 8)
    return {
        "activations": gaussian(key_of[0], (LENGTH, C), 1.0, 6.0, ((0, 128),)),
        "conv_weight": gaussian(key_of[1], (LAYERS, 3, C, C), (3 * C) ** -0.5, 0.1875),
        "conv_bias": gaussian(key_of[2], (LAYERS, C), 0.5, 3.0, (), jnp.float32),
        "conv_gain": jnp.clip(1.0 + 0.18 * jax.random.normal(key_of[3], (LAYERS, C), jnp.float32), 0.1, 1.9),
        "mlp_gain": jnp.clip(1.0 + 0.18 * jax.random.normal(key_of[4], (LAYERS, C), jnp.float32), 0.1, 1.9),
        "w_in": gaussian(key_of[5], (LAYERS, C, HID), C ** -0.5, 0.3125),
        "w_out": gaussian(key_of[6], (LAYERS, HID, C), HID ** -0.5, 0.21875),
    }


def rms_scale(values, gain):
    wide = values.astype(jnp.float32)
    inverse = jax.lax.rsqrt(lax.optimization_barrier(jnp.mean(wide * wide, axis=-1, keepdims=True)) + 1e-06)
    return (wide * inverse * gain[None, :]).astype(jnp.bfloat16)

def reference(activations, conv_weight, conv_bias, conv_gain, mlp_gain, w_in, w_out):
    state = activations
    for layer in range(LAYERS):
        span = S_DEV * 2 ** layer
        normed = rms_scale(state, conv_gain[layer])
        blank = jnp.zeros((span, C), jnp.bfloat16)
        earlier = jnp.concatenate([blank, normed[:-span]], axis=0)
        later = jnp.concatenate([normed[span:], blank], axis=0)
        pre = jnp.dot(earlier, conv_weight[layer, 0], preferred_element_type=jnp.float32)
        pre = pre + jnp.dot(normed, conv_weight[layer, 1], preferred_element_type=jnp.float32)
        pre = pre + jnp.dot(later, conv_weight[layer, 2], preferred_element_type=jnp.float32)
        pre = pre + conv_bias[layer][None, :]
        middle = (state.astype(jnp.float32) + jax.nn.gelu(pre, approximate=False)).astype(jnp.bfloat16)
        inner = rms_scale(middle, mlp_gain[layer])
        hidden = jax.nn.gelu(jnp.dot(inner, w_in[layer], preferred_element_type=jnp.float32), approximate=False).astype(jnp.bfloat16)
        state = (middle.astype(jnp.float32) + jnp.dot(hidden, w_out[layer], preferred_element_type=jnp.float32)).astype(jnp.bfloat16)
    return state.T
```

```python
import functools
import jax
import jax.numpy as jnp
from jax import lax
from jax.experimental import pallas as pl
from jax.experimental.pallas import tpu as pltpu
from jax.sharding import PartitionSpec as P

PAD = 8


def gelu(x):
    half = 0.5 * x
    return half + half * lax.erf(x * 0.7071067811865476)


def rms(wide, gain):
    inverse = lax.rsqrt(jnp.mean(wide * wide, axis=-1, keepdims=True) + 1e-06)
    return (wide * inverse * gain).astype(jnp.bfloat16)


def tower(state, normed, flat, packed, cw, cb, cg, mg, wi, wo, G, TB):
    nb, _, ch = state.shape
    layers = cw.shape[0]
    tiles = nb // TB

    def fill_pads(buf, d_blocks):
        if G == 16:
            zero = jnp.zeros((PAD, 16, ch), jnp.bfloat16)
            normed[buf, pl.ds(0, PAD)] = zero
            normed[buf, pl.ds(PAD + nb, PAD)] = zero
        else:
            tail = normed[buf, pl.ds(nb, PAD)].astype(jnp.float32)
            head = normed[buf, pl.ds(PAD, PAD)].astype(jnp.float32)
            zero = jnp.zeros((PAD, G, ch), jnp.float32)
            normed[buf, pl.ds(0, PAD)] = jnp.concatenate([zero, tail[:, : 16 - G]], axis=1).astype(jnp.bfloat16)
            normed[buf, pl.ds(PAD + nb, PAD)] = jnp.concatenate([head[:, G:], zero], axis=1).astype(jnp.bfloat16)

    def first(t, _):
        x = state[pl.ds(t * TB, TB)].reshape(TB * 16, ch).astype(jnp.float32)
        normed[0, pl.ds(PAD + t * TB, TB)] = rms(x, cg[0, :][None, :]).reshape(TB, 16, ch)
        return 0

    lax.fori_loop(0, tiles, first, 0)
    fill_pads(0, 1)

    def body(layer, t, last):
        cur = lax.rem(layer, 2)
        d = lax.shift_left(1, layer)
        b0 = PAD + t * TB
        lhs = jnp.concatenate(
            [normed[cur, pl.ds(b0 + s, TB)].reshape(TB * 16, ch) for s in (-d, 0, d)], axis=1
        )
        pre = jnp.dot(lhs, cw[layer], preferred_element_type=jnp.float32) + cb[layer, :][None, :]
        x = state[pl.ds(t * TB, TB)].reshape(TB * 16, ch).astype(jnp.float32)
        middle = (x + gelu(pre)).astype(jnp.bfloat16)
        wide = middle.astype(jnp.float32)
        inner = rms(wide, mg[layer, :][None, :])
        hidden = gelu(jnp.dot(inner, wi[layer], preferred_element_type=jnp.float32)).astype(jnp.bfloat16)
        out = wide + jnp.dot(hidden, wo[layer], preferred_element_type=jnp.float32)
        if last:
            for k in range(3):
                flat[k, pl.ds(t * TB * 16, TB * 16)] = out[:, k * 128 : (k + 1) * 128]
        else:
            new = out.astype(jnp.bfloat16)
            state[pl.ds(t * TB, TB)] = new.reshape(TB, 16, ch)
            normed[1 - cur, pl.ds(b0, TB)] = rms(new.astype(jnp.float32), cg[layer + 1, :][None, :]).reshape(TB, 16, ch)
        return 0

    def one_layer(layer, _):
        lax.fori_loop(0, tiles, lambda t, c: body(layer, t, False), 0)
        fill_pads(1 - lax.rem(layer, 2), 0)
        return 0

    lax.fori_loop(0, layers - 1, one_layer, 0)
    lax.fori_loop(0, tiles, lambda t, c: body(layers - 1, t, True), 0)


def emit(flat, turned, packed, G):
    nb = flat.shape[1] // 16
    for k in range(3):
        for o in range(G):
            rows = [flat[k, pl.ds(f * G + o, nb, stride=16), :] for f in range(16 // G)]
            block = rows[0] if len(rows) == 1 else jnp.concatenate(rows, axis=0)
            turned[pl.ds(k * 128 * G + o, 128, stride=G), :] = block.T
    n = packed.shape[0]
    step = 8

    def cast(g, _):
        values = turned[pl.ds(pl.multiple_of(g * step * 3 * G, 8), step * 3 * G), :]
        packed[pl.ds(g * step, step)] = values.astype(jnp.bfloat16).reshape(step, 3 * G, 128)
        return 0

    lax.fori_loop(0, n // step, cast, 0)


def kernel(x_hbm, cw_hbm, cb, cg, mg, wi_hbm, wo_hbm, out_ref, state, normed, flat, turned, cw, wi, wo, sem, *, G, TB):
    loads = [
        pltpu.make_async_copy(s, d, sem.at[n])
        for n, (s, d) in enumerate(((x_hbm, state), (cw_hbm, cw), (wi_hbm, wi), (wo_hbm, wo)))
    ]
    for load in loads:
        load.start()
    for load in loads:
        load.wait()
    tower(state, normed, flat, None, cw, cb, cg, mg, wi, wo, G, TB)
    emit(flat, turned, out_ref, G)


def shards(activations, conv_weight, conv_bias, conv_gain, mlp_gain, w_in, w_out):
    n = lax.axis_size("seq")
    rows, ch = activations.shape
    layers = conv_weight.shape[0]
    hid = w_in.shape[2]
    G = rows // n
    taps = conv_weight.reshape(layers, 3 * ch, ch)
    mine = lax.all_to_all(activations, "seq", split_axis=0, concat_axis=0, tiled=True)
    vm = pl.BlockSpec(memory_space=pltpu.VMEM)
    hbm = pl.BlockSpec(memory_space=pl.ANY)
    packed = pl.pallas_call(
        functools.partial(kernel, G=G, TB=16),
        out_shape=jax.ShapeDtypeStruct((n, 3 * G, n), jnp.bfloat16),
        in_specs=[hbm, hbm, vm, vm, vm, hbm, hbm],
        out_specs=vm,
        scratch_shapes=[
            pltpu.VMEM((n * G // 16, 16, ch), jnp.bfloat16),
            pltpu.VMEM((2, n * G // 16 + 2 * PAD, 16, ch), jnp.bfloat16),
            pltpu.VMEM((3, n * G, 128), jnp.float32),
            pltpu.VMEM((ch * G, 128), jnp.float32),
            pltpu.VMEM((layers, 3 * ch, ch), jnp.bfloat16),
            pltpu.VMEM((layers, ch, hid), jnp.bfloat16),
            pltpu.VMEM((layers, hid, ch), jnp.bfloat16),
            pltpu.SemaphoreType.DMA((4,)),
        ],
        compiler_params=pltpu.CompilerParams(vmem_limit_bytes=56 * 1024 * 1024),
    )(mine.reshape(n * G // 16, 16, ch), taps, conv_bias, conv_gain, mlp_gain, w_in, w_out)
    got = lax.all_to_all(packed, "seq", split_axis=0, concat_axis=0, tiled=True)
    return got.reshape(n, 3, G, n).transpose(1, 3, 0, 2).reshape(3, n * n * G)


def solution(mesh):
    in_specs = (P("seq", None), P(), P(), P(), P(), P(), P())
    out_specs = P("seq", None)
    return jax.shard_map(shards, mesh=mesh, in_specs=in_specs, out_specs=out_specs, check_vma=False)
```

```python
import functools

import jax
import jax.numpy as jnp
from jax import lax
from jax.experimental import pallas as pl
from jax.experimental.pallas import tpu as pltpu
from jax.sharding import PartitionSpec as P

PAD = 8
G = 8
SEG = 16 // G
TB = 16
STRIDE = 37
MESH = pl.DeviceIdType.MESH


def gelu(x):
    half = 0.5 * x
    return half + half * lax.erf(x * 0.7071067811865476)


def rms(wide, gain):
    inverse = lax.rsqrt(jnp.mean(wide * wide, axis=-1, keepdims=True) + 1e-06)
    return (wide * inverse * gain).astype(jnp.bfloat16)


def tower(c, state, normed, flat, cw, cb, cg, mg, wi, wo):
    nb, ch = state.shape[1], state.shape[-1]
    layers = cw.shape[0]
    tiles = nb // TB

    def rows_of(t):
        return state[c, pl.ds(t * TB, TB)].reshape(TB * 16, ch)

    def fill_pads(buf):
        tail = normed[buf, pl.ds(nb, PAD)].astype(jnp.float32)
        head = normed[buf, pl.ds(PAD, PAD)].astype(jnp.float32)
        zero = jnp.zeros((PAD, G, ch), jnp.float32)
        normed[buf, pl.ds(0, PAD)] = jnp.concatenate([zero, tail[:, : 16 - G]], axis=1).astype(jnp.bfloat16)
        normed[buf, pl.ds(PAD + nb, PAD)] = jnp.concatenate([head[:, G:], zero], axis=1).astype(jnp.bfloat16)

    def first(t, carry):
        x = rows_of(t).astype(jnp.float32)
        normed[0, pl.ds(PAD + t * TB, TB)] = rms(x, cg[0, :][None, :]).reshape(TB, 16, ch)
        return carry

    lax.fori_loop(0, tiles, first, 0)
    fill_pads(0)

    def body(layer, t, last):
        cur = lax.rem(layer, 2)
        d = lax.shift_left(1, layer)
        b0 = PAD + t * TB
        lhs = jnp.concatenate(
            [normed[cur, pl.ds(b0 + s, TB)].reshape(TB * 16, ch) for s in (-d, 0, d)], axis=1
        )
        pre = jnp.dot(lhs, cw[layer], preferred_element_type=jnp.float32) + cb[layer, :][None, :]
        middle = (rows_of(t).astype(jnp.float32) + gelu(pre)).astype(jnp.bfloat16)
        wide = middle.astype(jnp.float32)
        inner = rms(wide, mg[layer, :][None, :])
        hidden = gelu(jnp.dot(inner, wi[layer], preferred_element_type=jnp.float32)).astype(jnp.bfloat16)
        out = wide + jnp.dot(hidden, wo[layer], preferred_element_type=jnp.float32)
        if last:
            for k in range(ch // 128):
                flat[k, pl.ds(t * TB * 16, TB * 16)] = out[:, k * 128 : (k + 1) * 128]
        else:
            new = out.astype(jnp.bfloat16)
            state[c, pl.ds(t * TB, TB)] = new.reshape(TB, SEG, G, ch)
            scaled = rms(new.astype(jnp.float32), cg[layer + 1, :][None, :])
            normed[1 - cur, pl.ds(b0, TB)] = scaled.reshape(TB, 16, ch)
        return 0

    def one_layer(layer, carry):
        lax.fori_loop(0, tiles, lambda t, x: body(layer, t, False), 0)
        fill_pads(1 - lax.rem(layer, 2))
        return carry

    lax.fori_loop(0, layers - 1, one_layer, 0)
    lax.fori_loop(0, tiles, lambda t, x: body(layers - 1, t, True), 0)


def emit(c, flat, turned, packed):
    nb = flat.shape[1] // 16
    for k in range(flat.shape[0]):
        for o in range(G):
            rows = [flat[k, pl.ds(f * G + o, nb, stride=16), :] for f in range(SEG)]
            block = jnp.concatenate(rows, axis=0)
            turned[pl.ds(k * 128 * G + o, 128, stride=G), :] = block.T
    step, per = 8, packed.shape[2]

    def cast(g, carry):
        values = turned[pl.ds(pl.multiple_of(g * step * per, 8), step * per), :]
        packed[c, pl.ds(g * step, step)] = values.astype(jnp.bfloat16).reshape(step, per, 128)
        return carry

    lax.fori_loop(0, packed.shape[1] // step, cast, 0)


def move_kernel(
    x_hbm, cw_hbm, cb, cg, mg, wi_hbm, wo_hbm, got,
    state, normed, flat, turned, packed, cw, wi, wo,
    load_sem, in_send, in_recv, out_send, out_recv,
):
    me = lax.axis_index("seq")
    chunks, n = packed.shape[0], packed.shape[1]
    nb = state.shape[1]
    loads = [
        pltpu.make_async_copy(s, d, load_sem.at[k])
        for k, (s, d) in enumerate(((cw_hbm, cw), (wi_hbm, wi), (wo_hbm, wo)))
    ]
    for load in loads:
        load.start()

    def peer_of(q):
        p = lax.rem(q * STRIDE, n)
        core = lax.rem(me + p, 2)
        y = lax.rem(me // 2 + p // 2, 4)
        z = lax.rem(me // 8 + p // 8, 4)
        x = lax.rem(me // 32 + p // 32, 4)
        return ((x * 4 + z) * 4 + y) * 2 + core

    barrier = pltpu.get_barrier_semaphore()

    def greet(q, carry):
        pl.semaphore_signal(barrier, inc=1, device_id=(peer_of(q),), device_id_type=MESH)
        return carry

    lax.fori_loop(1, n, greet, 0)
    pl.semaphore_wait(barrier, n - 1)

    def source(c, j):
        return x_hbm.at[pl.ds(pl.multiple_of((c * n + j) * G, 8), G)]

    home = lax.rem(me, nb), me // nb
    for c in range(chunks):
        place = state.at[c, home[0], home[1]]
        pltpu.make_async_copy(source(c, me), place, in_recv.at[c]).start()

        def send(q, carry):
            j = peer_of(q)
            pltpu.make_async_remote_copy(
                source(c, j), place, in_send.at[c], in_recv.at[c], device_id=(j,), device_id_type=MESH
            ).start()
            return carry

        lax.fori_loop(1, n, send, 0)
    for load in loads:
        load.wait()

    def one_chunk(c, carry):
        pltpu.make_async_copy(state.at[c], state.at[c], in_recv.at[c]).wait()
        tower(c, state, normed, flat, cw, cb, cg, mg, wi, wo)
        emit(c, flat, turned, packed)
        pltpu.make_async_copy(packed.at[c, me], got.at[c, me], out_recv.at[c]).start()

        def send(q, x):
            j = peer_of(q)
            pltpu.make_async_remote_copy(
                packed.at[c, j], got.at[c, me], out_send.at[c], out_recv.at[c],
                device_id=(j,), device_id_type=MESH,
            ).start()
            return x

        lax.fori_loop(1, n, send, 0)
        return carry

    lax.fori_loop(0, chunks, one_chunk, 0)
    for c in range(chunks):
        sent = x_hbm.at[pl.ds(0, (n - 1) * G)]
        pltpu.make_async_copy(sent, sent, in_send.at[c]).wait()
        sent = packed.at[c, pl.ds(0, n - 1)]
        pltpu.make_async_copy(sent, sent, out_send.at[c]).wait()
        pltpu.make_async_copy(got.at[c], got.at[c], out_recv.at[c]).wait()


def turn_kernel(got, out_ref, wide):
    chunks, n = got.shape[0], got.shape[1]
    per = 128 // G
    blocks = n // per
    total = chunks * blocks
    for r in range(3):
        def one(b, carry):
            c, g = b // blocks, lax.rem(b, blocks)
            tile = got[c, pl.ds(g * per, per), pl.ds(r * G, G), :].reshape(128, n).astype(jnp.float32)
            wide[pl.ds(b * 4 + r, n, stride=4 * total), :] = tile.T
            return carry

        lax.fori_loop(0, total, one, 0)

    def store(i, carry):
        base = pl.multiple_of(i * total * 4, 4)
        row = jnp.concatenate([wide[pl.ds(base + 4 * b, 4), :] for b in range(total)], axis=1)
        out_ref[:, pl.ds(pl.multiple_of(i * total * 128, 128), total * 128)] = row[:3].astype(jnp.bfloat16)
        return carry

    lax.fori_loop(0, n, store, 0)


def shards(activations, conv_weight, conv_bias, conv_gain, mlp_gain, w_in, w_out):
    n = lax.axis_size("seq")
    rows, ch = activations.shape
    layers = conv_weight.shape[0]
    hid = w_in.shape[2]
    chunks = rows // (n * G)
    nb = n // SEG
    own = ch // n
    taps = conv_weight.reshape(layers, 3 * ch, ch)
    vm = pl.BlockSpec(memory_space=pltpu.VMEM)
    hbm = pl.BlockSpec(memory_space=pl.ANY)
    got = pl.pallas_call(
        move_kernel,
        out_shape=jax.ShapeDtypeStruct((chunks, n, own * G, n), jnp.bfloat16),
        in_specs=[hbm, hbm, vm, vm, vm, hbm, hbm],
        out_specs=hbm,
        scratch_shapes=[
            pltpu.VMEM((chunks, nb, SEG, G, ch), jnp.bfloat16),
            pltpu.VMEM((2, nb + 2 * PAD, 16, ch), jnp.bfloat16),
            pltpu.VMEM((ch // 128, n * G, 128), jnp.float32),
            pltpu.VMEM((ch * G, 128), jnp.float32),
            pltpu.VMEM((chunks, n, own * G, n), jnp.bfloat16),
            pltpu.VMEM((layers, 3 * ch, ch), jnp.bfloat16),
            pltpu.VMEM((layers, ch, hid), jnp.bfloat16),
            pltpu.VMEM((layers, hid, ch), jnp.bfloat16),
            pltpu.SemaphoreType.DMA((3,)),
            pltpu.SemaphoreType.DMA((chunks,)),
            pltpu.SemaphoreType.DMA((chunks,)),
            pltpu.SemaphoreType.DMA((chunks,)),
            pltpu.SemaphoreType.DMA((chunks,)),
        ],
        compiler_params=pltpu.CompilerParams(
            vmem_limit_bytes=40 * 1024 * 1024, collective_id=0, has_side_effects=True
        ),
    )(activations, taps, conv_bias, conv_gain, mlp_gain, w_in, w_out)
    return pl.pallas_call(
        turn_kernel,
        out_shape=jax.ShapeDtypeStruct((own, n * rows), jnp.bfloat16),
        in_specs=[vm],
        out_specs=vm,
        scratch_shapes=[pltpu.VMEM((n * rows // 128 * 4, 128), jnp.float32)],
        compiler_params=pltpu.CompilerParams(vmem_limit_bytes=40 * 1024 * 1024),
    )(got)


def solution(mesh):
    in_specs = (P("seq", None), P(), P(), P(), P(), P(), P())
    out_specs = P("seq", None)
    return jax.shard_map(shards, mesh=mesh, in_specs=in_specs, out_specs=out_specs, check_vma=False)
```

```python
import functools

import jax
import jax.numpy as jnp
from jax import lax
from jax.experimental import pallas as pl
from jax.experimental.pallas import tpu as pltpu
from jax.sharding import PartitionSpec as P

PAD = 8
G = 8
SEG = 16 // G
TB = 64
STRIDE = 37
VMEM = 63 * 1024 * 1024
MESH = pl.DeviceIdType.MESH


def gelu(x):
    half = 0.5 * x
    return half + half * lax.erf(x * 0.7071067811865476)


def rms(wide, gain):
    inverse = lax.rsqrt(jnp.mean(wide * wide, axis=-1, keepdims=True) + 1e-06)
    return (wide * inverse * gain).astype(jnp.bfloat16)


def tower(c, state, normed, flat, cw, cb, cg, mg, wi, wo):
    nb, ch = state.shape[1], state.shape[-1]
    layers = cw.shape[0]
    tiles = nb // TB

    def rows_of(t):
        return state[c, pl.ds(t * TB, TB)].reshape(TB * 16, ch)

    def fill_pads(buf):
        tail = normed[buf, pl.ds(nb, PAD)].astype(jnp.float32)
        head = normed[buf, pl.ds(PAD, PAD)].astype(jnp.float32)
        zero = jnp.zeros((PAD, G, ch), jnp.float32)
        normed[buf, pl.ds(0, PAD)] = jnp.concatenate([zero, tail[:, : 16 - G]], axis=1).astype(jnp.bfloat16)
        normed[buf, pl.ds(PAD + nb, PAD)] = jnp.concatenate([head[:, G:], zero], axis=1).astype(jnp.bfloat16)

    def first(t, carry):
        x = rows_of(t).astype(jnp.float32)
        normed[0, pl.ds(PAD + t * TB, TB)] = rms(x, cg[0, :][None, :]).reshape(TB, 16, ch)
        return carry

    lax.fori_loop(0, tiles, first, 0)
    fill_pads(0)

    def body(layer, t, last):
        cur = lax.rem(layer, 2)
        d = lax.shift_left(1, layer)
        b0 = PAD + t * TB
        lhs = jnp.concatenate(
            [normed[cur, pl.ds(b0 + s, TB)].reshape(TB * 16, ch) for s in (-d, 0, d)], axis=1
        )
        pre = jnp.dot(lhs, cw[layer], preferred_element_type=jnp.float32) + cb[layer, :][None, :]
        middle = (rows_of(t).astype(jnp.float32) + gelu(pre)).astype(jnp.bfloat16)
        wide = middle.astype(jnp.float32)
        inner = rms(wide, mg[layer, :][None, :])
        hidden = gelu(jnp.dot(inner, wi[layer], preferred_element_type=jnp.float32)).astype(jnp.bfloat16)
        out = wide + jnp.dot(hidden, wo[layer], preferred_element_type=jnp.float32)
        if last:
            for k in range(ch // 128):
                flat[k, pl.ds(t * TB * 16, TB * 16)] = out[:, k * 128 : (k + 1) * 128]
        else:
            new = out.astype(jnp.bfloat16)
            state[c, pl.ds(t * TB, TB)] = new.reshape(TB, SEG, G, ch)
            scaled = rms(new.astype(jnp.float32), cg[layer + 1, :][None, :])
            normed[1 - cur, pl.ds(b0, TB)] = scaled.reshape(TB, 16, ch)
        return 0

    def one_layer(layer, carry):
        lax.fori_loop(0, tiles, lambda t, x: body(layer, t, False), 0)
        fill_pads(1 - lax.rem(layer, 2))
        return carry

    lax.fori_loop(0, layers - 1, one_layer, 0)
    lax.fori_loop(0, tiles, lambda t, x: body(layers - 1, t, True), 0)


def emit(c, flat, turned, packed):
    nb = flat.shape[1] // 16
    for k in range(flat.shape[0]):
        for o in range(G):
            rows = [flat[k, pl.ds(f * G + o, nb, stride=16), :] for f in range(SEG)]
            block = jnp.concatenate(rows, axis=0)
            turned[pl.ds(k * 128 * G + o, 128, stride=G), :] = block.T
    step, per = 8, packed.shape[2]

    def cast(g, carry):
        values = turned[pl.ds(pl.multiple_of(g * step * per, 8), step * per), :]
        packed[c, pl.ds(g * step, step)] = values.astype(jnp.bfloat16).reshape(step, per, 128)
        return carry

    lax.fori_loop(0, packed.shape[1] // step, cast, 0)


def move_kernel(
    x_hbm, cw_hbm, cb, cg, mg, wi_hbm, wo_hbm, got,
    state, normed, flat, turned, packed, cw, wi, wo,
    load_sem, in_send, in_recv, out_send, out_recv,
):
    me = lax.axis_index("seq")
    chunks, n = packed.shape[0], packed.shape[1]
    nb = state.shape[1]
    loads = [
        pltpu.make_async_copy(s, d, load_sem.at[k])
        for k, (s, d) in enumerate(((cw_hbm, cw), (wi_hbm, wi), (wo_hbm, wo)))
    ]
    for load in loads:
        load.start()

    def peer_of(q):
        p = lax.rem(q * STRIDE, n)
        core = lax.rem(me + p, 2)
        y = lax.rem(me // 2 + p // 2, 4)
        z = lax.rem(me // 8 + p // 8, 4)
        x = lax.rem(me // 32 + p // 32, 4)
        return ((x * 4 + z) * 4 + y) * 2 + core

    barrier = pltpu.get_barrier_semaphore()

    def greet(q, carry):
        pl.semaphore_signal(barrier, inc=1, device_id=(peer_of(q),), device_id_type=MESH)
        return carry

    lax.fori_loop(1, n, greet, 0)
    pl.semaphore_wait(barrier, n - 1)

    def source(c, j):
        return x_hbm.at[pl.ds(pl.multiple_of((c * n + j) * G, 8), G)]

    home = lax.rem(me, nb), me // nb
    for c in range(chunks):
        place = state.at[c, home[0], home[1]]
        pltpu.make_async_copy(source(c, me), place, in_recv.at[c]).start()

        def send(q, carry):
            j = peer_of(q)
            pltpu.make_async_remote_copy(
                source(c, j), place, in_send.at[c], in_recv.at[c], device_id=(j,), device_id_type=MESH
            ).start()
            return carry

        lax.fori_loop(1, n, send, 0)
    for load in loads:
        load.wait()

    def one_chunk(c, carry):
        pltpu.make_async_copy(state.at[c], state.at[c], in_recv.at[c]).wait()
        tower(c, state, normed, flat, cw, cb, cg, mg, wi, wo)
        emit(c, flat, turned, packed)
        pltpu.make_async_copy(packed.at[c, me], got.at[c, me], out_recv.at[c]).start()

        def send(q, x):
            j = peer_of(q)
            pltpu.make_async_remote_copy(
                packed.at[c, j], got.at[c, me], out_send.at[c], out_recv.at[c],
                device_id=(j,), device_id_type=MESH,
            ).start()
            return x

        lax.fori_loop(1, n, send, 0)
        return carry

    lax.fori_loop(0, chunks, one_chunk, 0)
    for c in range(chunks):
        sent = x_hbm.at[pl.ds(0, (n - 1) * G)]
        pltpu.make_async_copy(sent, sent, in_send.at[c]).wait()
        sent = packed.at[c, pl.ds(0, n - 1)]
        pltpu.make_async_copy(sent, sent, out_send.at[c]).wait()
        pltpu.make_async_copy(got.at[c], got.at[c], out_recv.at[c]).wait()


def turn_kernel(got_hbm, out_hbm, got, wide, out, load_sem, out_sem):
    chunks, n = got.shape[0], got.shape[1]
    per = 128 // G
    total = chunks * n // per
    quarter = n // 4
    loads = {}
    for c in range(chunks):
        for h in range(4):
            part = c, pl.ds(h * quarter, quarter)
            loads[c, h] = pltpu.make_async_copy(got_hbm.at[part], got.at[part], load_sem.at[c, h])
            loads[c, h].start()
    for b in range(total):
        c, j = b // (n // per), b % (n // per) * per
        if j % quarter == 0:
            loads[c, j // quarter].wait()
        for r in range(3):
            tile = got[c, pl.ds(j, per), pl.ds(r * G, G), :].reshape(128, n).astype(jnp.float32)
            wide[pl.ds(b * 4 + r, n, stride=4 * total), :] = tile.T

    width = total * 128
    stores = []
    for h in range(4):
        def store(g, carry):
            for k in range(4):
                i = h * quarter + g * 4 + k
                base = pl.multiple_of(i * total * 4, 4)
                row = jnp.concatenate([wide[pl.ds(base + 4 * b, 4), :] for b in range(total)], axis=1)
                out[:, pl.ds(pl.multiple_of(i * width, 128), width)] = row[:3].astype(jnp.bfloat16)
            return carry

        lax.fori_loop(0, quarter // 4, store, 0)
        part = slice(None), pl.ds(h * quarter * width, quarter * width)
        stores.append(pltpu.make_async_copy(out.at[part], out_hbm.at[part], out_sem.at[h]))
        stores[-1].start()
    for copy in stores:
        copy.wait()


def shards(activations, conv_weight, conv_bias, conv_gain, mlp_gain, w_in, w_out):
    n = lax.axis_size("seq")
    rows, ch = activations.shape
    layers = conv_weight.shape[0]
    hid = w_in.shape[2]
    chunks = rows // (n * G)
    nb = n // SEG
    own = ch // n
    taps = conv_weight.reshape(layers, 3 * ch, ch)
    vm = pl.BlockSpec(memory_space=pltpu.VMEM)
    hbm = pl.BlockSpec(memory_space=pl.ANY)
    got = pl.pallas_call(
        move_kernel,
        out_shape=jax.ShapeDtypeStruct((chunks, n, own * G, n), jnp.bfloat16),
        in_specs=[hbm, hbm, vm, vm, vm, hbm, hbm],
        out_specs=hbm,
        scratch_shapes=[
            pltpu.VMEM((chunks, nb, SEG, G, ch), jnp.bfloat16),
            pltpu.VMEM((2, nb + 2 * PAD, 16, ch), jnp.bfloat16),
            pltpu.VMEM((ch // 128, n * G, 128), jnp.float32),
            pltpu.VMEM((ch * G, 128), jnp.float32),
            pltpu.VMEM((chunks, n, own * G, n), jnp.bfloat16),
            pltpu.VMEM((layers, 3 * ch, ch), jnp.bfloat16),
            pltpu.VMEM((layers, ch, hid), jnp.bfloat16),
            pltpu.VMEM((layers, hid, ch), jnp.bfloat16),
            pltpu.SemaphoreType.DMA((3,)),
            pltpu.SemaphoreType.DMA((chunks,)),
            pltpu.SemaphoreType.DMA((chunks,)),
            pltpu.SemaphoreType.DMA((chunks,)),
            pltpu.SemaphoreType.DMA((chunks,)),
        ],
        compiler_params=pltpu.CompilerParams(
            vmem_limit_bytes=VMEM, collective_id=0, has_side_effects=True
        ),
    )(activations, taps, conv_bias, conv_gain, mlp_gain, w_in, w_out)
    return pl.pallas_call(
        turn_kernel,
        out_shape=jax.ShapeDtypeStruct((own, n * rows), jnp.bfloat16),
        in_specs=[hbm],
        out_specs=hbm,
        scratch_shapes=[
            pltpu.VMEM((chunks, n, own * G, n), jnp.bfloat16),
            pltpu.VMEM((n * rows // 128 * 4, 128), jnp.float32),
            pltpu.VMEM((own, n * rows), jnp.bfloat16),
            pltpu.SemaphoreType.DMA((chunks, 4)),
            pltpu.SemaphoreType.DMA((4,)),
        ],
        compiler_params=pltpu.CompilerParams(vmem_limit_bytes=VMEM),
    )(got)


def solution(mesh):
    in_specs = (P("seq", None), P(), P(), P(), P(), P(), P())
    out_specs = P("seq", None)
    return jax.shard_map(shards, mesh=mesh, in_specs=in_specs, out_specs=out_specs, check_vma=False)
```

```python
import functools

import jax
import jax.numpy as jnp
from jax import lax
from jax.experimental import pallas as pl
from jax.experimental.pallas import tpu as pltpu
from jax.sharding import PartitionSpec as P

PAD = 8
G = 4
SEG = 16 // G
GROUPS = ((0,), (1, 2), (3,))
VMEM = 63 * 1024 * 1024
MESH = pl.DeviceIdType.MESH


def gelu(x):
    half = 0.5 * x
    return half + half * lax.erf(x * 0.7071067811865476)


def rms(wide, gain):
    inverse = lax.rsqrt(jnp.mean(wide * wide, axis=-1, keepdims=True) + 1e-06)
    return (wide * inverse * gain).astype(jnp.bfloat16)


def tower(group, state, normed, flat, cw, cb, cg, mg, wi, wo):
    nb, ch = state.shape[1], state.shape[-1]
    layers = cw.shape[0]
    k = len(group)
    rows = k * nb * 16
    own, subs = pl.ds(group[0], k), pl.ds(0, k)

    def load():
        return state[own].reshape(rows, ch).astype(jnp.float32)

    def put(buf, wide, gain):
        normed[buf, subs, pl.ds(PAD, nb)] = rms(wide, gain[None, :]).reshape(k, nb, 16, ch)
        tail = normed[buf, subs, pl.ds(nb, PAD)].astype(jnp.float32)
        head = normed[buf, subs, pl.ds(PAD, PAD)].astype(jnp.float32)
        zero = jnp.zeros((k, PAD, G, ch), jnp.float32)
        normed[buf, subs, pl.ds(0, PAD)] = jnp.concatenate([zero, tail[:, :, : 16 - G]], axis=2).astype(jnp.bfloat16)
        normed[buf, subs, pl.ds(PAD + nb, PAD)] = jnp.concatenate([head[:, :, G:], zero], axis=2).astype(jnp.bfloat16)

    def body(layer, last):
        cur = lax.rem(layer, 2)
        d = lax.shift_left(1, layer)
        lhs = jnp.concatenate(
            [normed[cur, subs, pl.ds(PAD + s, nb)].reshape(rows, ch) for s in (-d, 0, d)], axis=1
        )
        pre = jnp.dot(lhs, cw[layer], preferred_element_type=jnp.float32) + cb[layer, :][None, :]
        middle = (load() + gelu(pre)).astype(jnp.bfloat16)
        wide = middle.astype(jnp.float32)
        inner = rms(wide, mg[layer, :][None, :])
        hidden = gelu(jnp.dot(inner, wi[layer], preferred_element_type=jnp.float32)).astype(jnp.bfloat16)
        out = wide + jnp.dot(hidden, wo[layer], preferred_element_type=jnp.float32)
        if last:
            for j in range(ch // 128):
                flat[j, pl.ds(0, rows)] = out[:, j * 128 : (j + 1) * 128]
        else:
            new = out.astype(jnp.bfloat16)
            state[own] = new.reshape(k, nb, 16, ch)
            put(1 - cur, new.astype(jnp.float32), cg[layer + 1, :])

    def one_layer(layer, carry):
        body(layer, False)
        return carry

    put(0, load(), cg[0, :])
    lax.fori_loop(0, layers - 1, one_layer, 0)
    body(layers - 1, True)


def emit(part, base, flat, turned, packed, nb):
    pair, h = part // 2, part % 2
    for k in range(flat.shape[0]):
        for o in range(G):
            rows = [flat[k, pl.ds(base + f * G + o, nb, stride=16), :] for f in range(SEG)]
            turned[pl.ds(k * 128 * G + o, 128, stride=G), :] = jnp.concatenate(rows, axis=0).T
    own, step = packed.shape[2], 16

    def cast(g, carry):
        values = turned[pl.ds(pl.multiple_of(g * step * own * G, 8), step * own * G), :]
        packed[pair, pl.ds(g * step, step), :, pl.ds(h * G, G)] = values.astype(jnp.bfloat16).reshape(step, own, G, 128)
        return carry

    lax.fori_loop(0, packed.shape[1] // step, cast, 0)


def move_kernel(
    x_hbm, cw_hbm, cb, cg, mg, wi_hbm, wo_hbm, got,
    state, normed, flat, turned, packed, cw, wi, wo,
    load_sem, in_send, in_recv, out_send, out_recv,
):
    me = lax.axis_index("seq")
    pairs, n = packed.shape[0], packed.shape[1]
    parts, nb = state.shape[0], state.shape[1]
    loads = [
        pltpu.make_async_copy(s, d, load_sem.at[k])
        for k, (s, d) in enumerate(((cw_hbm, cw), (wi_hbm, wi), (wo_hbm, wo)))
    ]
    for load in loads:
        load.start()

    xs = [lax.rem(me // 32 + k, 4) * 32 for k in range(4)]
    cores = [lax.rem(me + k, 2) for k in range(2)]
    ends = [x + core for x in xs for core in cores]
    z_me, y_me = lax.rem(me // 8, 4), lax.rem(me // 2, 4)

    def each_peer(act):
        for end in ends[1:]:
            act(end + z_me * 8 + y_me * 2)

        def step(g, carry):
            y = lax.rem(g, 4)
            z = lax.rem(g // 4 + y, 4)
            middle = lax.rem(z_me + z, 4) * 8 + lax.rem(y_me + y, 4) * 2
            for end in ends:
                act(end + middle)
            return carry

        lax.fori_loop(1, n // len(ends), step, 0)

    barrier = pltpu.get_barrier_semaphore()
    each_peer(lambda j: pl.semaphore_signal(barrier, inc=1, device_id=(j,), device_id_type=MESH))
    pl.semaphore_wait(barrier, n - 1)

    for part in range(parts):
        pair, h = part // 2, part % 2
        place = state.at[part, lax.rem(me, nb), pl.ds(me // nb * G, G)]

        def source(j):
            return x_hbm.at[pl.ds((pair * n + j) * 2 * G + h * G, G)]

        pltpu.make_async_copy(source(me), place, in_recv.at[part]).start()
        each_peer(
            lambda j: pltpu.make_async_remote_copy(
                source(j), place, in_send.at[pair], in_recv.at[part], device_id=(j,), device_id_type=MESH
            ).start()
        )
    for load in loads:
        load.wait()

    for group in GROUPS:
        for part in group:
            pltpu.make_async_copy(state.at[part], state.at[part], in_recv.at[part]).wait()
        tower(group, state, normed, flat, cw, cb, cg, mg, wi, wo)
        for at, part in enumerate(group):
            emit(part, at * nb * 16, flat, turned, packed, nb)
            pair, rows = part // 2, pl.ds(part % 2 * G, G)
            place = got.at[pair, me, :, rows]
            pltpu.make_async_copy(packed.at[pair, me, :, rows], place, out_recv.at[pair]).start()
            each_peer(
                lambda j: pltpu.make_async_remote_copy(
                    packed.at[pair, j, :, rows], place, out_send.at[pair], out_recv.at[pair],
                    device_id=(j,), device_id_type=MESH,
                ).start()
            )

    for pair in range(pairs):
        sent = x_hbm.at[pl.ds(0, (n - 1) * 2 * G)]
        pltpu.make_async_copy(sent, sent, in_send.at[pair]).wait()
        sent = packed.at[pair, pl.ds(0, n - 1)]
        pltpu.make_async_copy(sent, sent, out_send.at[pair]).wait()
        pltpu.make_async_copy(got.at[pair], got.at[pair], out_recv.at[pair]).wait()


def turn_kernel(got_hbm, out_hbm, got, wide, out, load_sem, out_sem):
    pairs, n = got.shape[0], got.shape[1]
    rows = got.shape[3]
    per = 128 // rows
    total = pairs * n // per
    quarter = n // 4
    loads = {}
    for c in range(pairs):
        for h in range(4):
            part = c, pl.ds(h * quarter, quarter)
            loads[c, h] = pltpu.make_async_copy(got_hbm.at[part], got.at[part], load_sem.at[c, h])
            loads[c, h].start()
    for b in range(total):
        c, j = b // (n // per), b % (n // per) * per
        if j % quarter == 0:
            loads[c, j // quarter].wait()
        for r in range(3):
            tile = got[c, pl.ds(j, per), r].reshape(128, n).astype(jnp.float32)
            wide[pl.ds(b * 4 + r, n, stride=4 * total), :] = tile.T

    width = total * 128
    stores = []
    for h in range(4):
        def store(g, carry):
            for k in range(4):
                i = h * quarter + g * 4 + k
                base = pl.multiple_of(i * total * 4, 4)
                row = jnp.concatenate([wide[pl.ds(base + 4 * b, 4), :] for b in range(total)], axis=1)
                out[:, pl.ds(pl.multiple_of(i * width, 128), width)] = row[:3].astype(jnp.bfloat16)
            return carry

        lax.fori_loop(0, quarter // 4, store, 0)
        part = slice(None), pl.ds(h * quarter * width, quarter * width)
        stores.append(pltpu.make_async_copy(out.at[part], out_hbm.at[part], out_sem.at[h]))
        stores[-1].start()
    for copy in stores:
        copy.wait()


def shards(activations, conv_weight, conv_bias, conv_gain, mlp_gain, w_in, w_out):
    n = lax.axis_size("seq")
    rows, ch = activations.shape
    layers = conv_weight.shape[0]
    hid = w_in.shape[2]
    parts = rows // (n * G)
    pairs = parts // 2
    nb = n // SEG
    own = ch // n
    taps = conv_weight.reshape(layers, 3 * ch, ch)
    vm = pl.BlockSpec(memory_space=pltpu.VMEM)
    hbm = pl.BlockSpec(memory_space=pl.ANY)
    widest = max(map(len, GROUPS))
    tiles = (pairs, n, own, 2 * G, n)
    got = pl.pallas_call(
        move_kernel,
        out_shape=jax.ShapeDtypeStruct(tiles, jnp.bfloat16),
        in_specs=[hbm, hbm, vm, vm, vm, hbm, hbm],
        out_specs=hbm,
        scratch_shapes=[
            pltpu.VMEM((parts, nb, 16, ch), jnp.bfloat16),
            pltpu.VMEM((2, widest, nb + 2 * PAD, 16, ch), jnp.bfloat16),
            pltpu.VMEM((ch // 128, widest * nb * 16, 128), jnp.float32),
            pltpu.VMEM((ch * G, 128), jnp.float32),
            pltpu.VMEM(tiles, jnp.bfloat16),
            pltpu.VMEM((layers, 3 * ch, ch), jnp.bfloat16),
            pltpu.VMEM((layers, ch, hid), jnp.bfloat16),
            pltpu.VMEM((layers, hid, ch), jnp.bfloat16),
            pltpu.SemaphoreType.DMA((3,)),
            pltpu.SemaphoreType.DMA((pairs,)),
            pltpu.SemaphoreType.DMA((parts,)),
            pltpu.SemaphoreType.DMA((pairs,)),
            pltpu.SemaphoreType.DMA((pairs,)),
        ],
        compiler_params=pltpu.CompilerParams(
            vmem_limit_bytes=VMEM, collective_id=0, has_side_effects=True
        ),
    )(activations, taps, conv_bias, conv_gain, mlp_gain, w_in, w_out)
    return pl.pallas_call(
        turn_kernel,
        out_shape=jax.ShapeDtypeStruct((own, n * rows), jnp.bfloat16),
        in_specs=[hbm],
        out_specs=hbm,
        scratch_shapes=[
            pltpu.VMEM(tiles, jnp.bfloat16),
            pltpu.VMEM((n * rows // 128 * 4, 128), jnp.float32),
            pltpu.VMEM((own, n * rows), jnp.bfloat16),
            pltpu.SemaphoreType.DMA((pairs, 4)),
            pltpu.SemaphoreType.DMA((4,)),
        ],
        compiler_params=pltpu.CompilerParams(vmem_limit_bytes=VMEM),
    )(got)


def solution(mesh):
    in_specs = (P("seq", None), P(), P(), P(), P(), P(), P())
    out_specs = P("seq", None)
    return jax.shard_map(shards, mesh=mesh, in_specs=in_specs, out_specs=out_specs, check_vma=False)
```

```python
import functools

import jax
import jax.numpy as jnp
from jax import lax
from jax.experimental import pallas as pl
from jax.experimental.pallas import tpu as pltpu
from jax.sharding import PartitionSpec as P

PAD = 8
PARTS = ((0, 0, 4), (1, 0, 8), (0, 4, 4))
VMEM = 63 * 1024 * 1024
MESH = pl.DeviceIdType.MESH


def gelu(x):
    half = 0.5 * x
    return half + half * lax.erf(x * 0.7071067811865476)


def rms(wide, gain):
    inverse = lax.rsqrt(jnp.mean(wide * wide, axis=-1, keepdims=True) + 1e-06)
    return (wide * inverse * gain).astype(jnp.bfloat16)


def tower(state, normed, flat, cw, cb, cg, mg, wi, wo, G):
    nb, _, ch = state.shape
    layers = cw.shape[0]
    rows = nb * 16

    def load():
        return state[...].reshape(rows, ch).astype(jnp.float32)

    def put(buf, wide, gain):
        normed[buf, pl.ds(PAD, nb)] = rms(wide, gain[None, :]).reshape(nb, 16, ch)
        tail = normed[buf, pl.ds(nb, PAD)].astype(jnp.float32)
        head = normed[buf, pl.ds(PAD, PAD)].astype(jnp.float32)
        zero = jnp.zeros((PAD, G, ch), jnp.float32)
        normed[buf, pl.ds(0, PAD)] = jnp.concatenate([zero, tail[:, : 16 - G]], axis=1).astype(jnp.bfloat16)
        normed[buf, pl.ds(PAD + nb, PAD)] = jnp.concatenate([head[:, G:], zero], axis=1).astype(jnp.bfloat16)

    def body(layer, last):
        cur = lax.rem(layer, 2)
        d = lax.shift_left(1, layer)
        lhs = jnp.concatenate([normed[cur, pl.ds(PAD + s, nb)].reshape(rows, ch) for s in (-d, 0, d)], axis=1)
        pre = jnp.dot(lhs, cw[layer], preferred_element_type=jnp.float32) + cb[layer, :][None, :]
        middle = (load() + gelu(pre)).astype(jnp.bfloat16)
        wide = middle.astype(jnp.float32)
        inner = rms(wide, mg[layer, :][None, :])
        hidden = gelu(jnp.dot(inner, wi[layer], preferred_element_type=jnp.float32)).astype(jnp.bfloat16)
        out = wide + jnp.dot(hidden, wo[layer], preferred_element_type=jnp.float32)
        if last:
            for j in range(ch // 128):
                flat[j, pl.ds(0, rows)] = out[:, j * 128 : (j + 1) * 128]
        else:
            new = out.astype(jnp.bfloat16)
            state[...] = new.reshape(nb, 16, ch)
            put(1 - cur, new.astype(jnp.float32), cg[layer + 1, :])

    def one_layer(layer, carry):
        body(layer, False)
        return carry

    put(0, load(), cg[0, :])
    lax.fori_loop(0, layers - 1, one_layer, 0)
    body(layers - 1, True)


def emit(part, flat, turned, packed, nb):
    pair, first, G = part
    for k in range(flat.shape[0]):
        for o in range(G):
            rows = [flat[k, pl.ds(f * G + o, nb, stride=16), :] for f in range(16 // G)]
            turned[pl.ds(k * 128 * G + o, 128, stride=G), :] = jnp.concatenate(rows, axis=0).T
    own, step = packed.shape[2], 64 // G

    def cast(g, carry):
        values = turned[pl.ds(pl.multiple_of(g * step * own * G, 8), step * own * G), :]
        packed[pair, pl.ds(g * step, step), :, pl.ds(first, G)] = values.astype(jnp.bfloat16).reshape(step, own, G, 128)
        return carry

    lax.fori_loop(0, packed.shape[1] // step, cast, 0)


def turn(got, wide, after=()):
    n, own, rows, _ = got.shape
    per = 128 // rows
    for b in range(n // per):
        if b < len(after):
            after[b].wait()
        for r in range(own):
            tile = got[pl.ds(b * per, per), r].reshape(128, n).astype(jnp.float32)
            wide[pl.ds(b * 4 + r, n, stride=4 * (n // per)), :] = tile.T


def turned_row(wide, i, blocks):
    base = pl.multiple_of(i * blocks * 4, 4)
    row = jnp.concatenate([wide[pl.ds(base + 4 * b, 4), :] for b in range(blocks)], axis=1)
    return row[:3].astype(jnp.bfloat16)


def move_kernel(
    x_hbm, cw_hbm, cb_hbm, cg_hbm, mg_hbm, wi_hbm, wo_hbm, got, half_hbm,
    state_a, state_b, state_c, normed, flat, turned, packed, got_b, wide, half, cw, cb, cg, mg, wi, wo,
    load_sem, in_send, in_recv, out_send, out_recv, half_sem,
):
    me = lax.axis_index("seq")
    n = packed.shape[1]
    states = state_a, state_b, state_c
    loads = [
        pltpu.make_async_copy(s, d, load_sem.at[k])
        for k, (s, d) in enumerate(
            ((cw_hbm, cw), (cb_hbm, cb), (cg_hbm, cg), (mg_hbm, mg), (wi_hbm, wi), (wo_hbm, wo))
        )
    ]
    for load in loads:
        load.start()

    xs = [lax.rem(me // 32 + k, 4) * 32 for k in range(4)]
    cores = [lax.rem(me + k, 2) for k in range(2)]
    ends = [x + core for x in xs for core in cores]
    z_me, y_me = lax.rem(me // 8, 4), lax.rem(me // 2, 4)

    def each_peer(act):
        for end in ends[1:]:
            act(end + z_me * 8 + y_me * 2)

        def step(g, carry):
            y = lax.rem(g, 4)
            z = lax.rem(g // 4 + y, 4)
            middle = lax.rem(z_me + z, 4) * 8 + lax.rem(y_me + y, 4) * 2
            for end in ends:
                act(end + middle)
            return carry

        lax.fori_loop(1, n // len(ends), step, 0)

    barrier = pltpu.get_barrier_semaphore()
    each_peer(lambda j: pl.semaphore_signal(barrier, inc=1, device_id=(j,), device_id_type=MESH))
    pl.semaphore_wait(barrier, n - 1)

    for k, (pair, first, G) in enumerate(PARTS):
        nb = states[k].shape[0]
        place = states[k].at[lax.rem(me, nb), pl.ds(me // nb * G, G)]

        def source(j):
            return x_hbm.at[pl.ds((pair * n + j) * 8 + first, G)]

        pltpu.make_async_copy(source(me), place, in_recv.at[k]).start()
        each_peer(
            lambda j: pltpu.make_async_remote_copy(
                source(j), place, in_send.at[pair], in_recv.at[k], device_id=(j,), device_id_type=MESH
            ).start()
        )
    for load in loads:
        load.wait()

    for k, part in enumerate(PARTS):
        pair, first, G = part
        state = states[k]
        pltpu.make_async_copy(state, state, in_recv.at[k]).wait()
        tower(state, normed, flat, cw, cb, cg, mg, wi, wo, G)
        emit(part, flat, turned, packed, state.shape[0])
        rows = pl.ds(first, G)
        place = (got_b if pair else got).at[me, :, rows]
        pltpu.make_async_copy(packed.at[pair, me, :, rows], place, out_recv.at[pair]).start()
        each_peer(
            lambda j: pltpu.make_async_remote_copy(
                packed.at[pair, j, :, rows], place, out_send.at[pair], out_recv.at[pair],
                device_id=(j,), device_id_type=MESH,
            ).start()
        )

    pltpu.make_async_copy(got_b, got_b, out_recv.at[1]).wait()
    turn(got_b, wide)
    blocks = n // 16
    width = blocks * 128

    def store(g, carry):
        for k in range(4):
            i = g * 4 + k
            half[:, pl.ds(pl.multiple_of(i * width, 128), width)] = turned_row(wide, i, blocks)
        return carry

    lax.fori_loop(0, n // 4, store, 0)
    out = pltpu.make_async_copy(half, half_hbm, half_sem)
    out.start()
    for pair in range(2):
        sent = x_hbm.at[pl.ds(0, (n - 1) * 8)]
        pltpu.make_async_copy(sent, sent, in_send.at[pair]).wait()
        sent = packed.at[pair, pl.ds(0, n - 1)]
        pltpu.make_async_copy(sent, sent, out_send.at[pair]).wait()
    out.wait()
    pltpu.make_async_copy(got, got, out_recv.at[0]).wait()


def turn_kernel(got_hbm, half_hbm, out_hbm, got, half, wide, out, load_sem, half_sem, out_sem):
    n = got.shape[0]
    quarter = n // 4
    loads = []
    for b in range(8):
        part = pl.ds(b * 16, 16)
        loads.append(pltpu.make_async_copy(got_hbm.at[part], got.at[part], load_sem.at[b]))
        loads[-1].start()
    other = pltpu.make_async_copy(half_hbm, half, half_sem)
    other.start()
    turn(got, wide, loads)
    other.wait()
    blocks = n // 16
    width = blocks * 128
    stores = []
    for h in range(4):
        def store(g, carry):
            for k in range(4):
                i = h * quarter + g * 4 + k
                base = pl.multiple_of(i * 2 * width, 128)
                out[:, pl.ds(base, width)] = turned_row(wide, i, blocks)
                out[:, pl.ds(base + width, width)] = half[:, pl.ds(pl.multiple_of(i * width, 128), width)]
            return carry

        lax.fori_loop(0, quarter // 4, store, 0)
        part = slice(None), pl.ds(h * quarter * 2 * width, quarter * 2 * width)
        stores.append(pltpu.make_async_copy(out.at[part], out_hbm.at[part], out_sem.at[h]))
        stores[-1].start()
    for copy in stores:
        copy.wait()


def shards(activations, conv_weight, conv_bias, conv_gain, mlp_gain, w_in, w_out):
    n = lax.axis_size("seq")
    rows, ch = activations.shape
    layers = conv_weight.shape[0]
    hid = w_in.shape[2]
    own = ch // n
    taps = conv_weight.reshape(layers, 3 * ch, ch)
    hbm = pl.BlockSpec(memory_space=pl.ANY)
    states = [pltpu.VMEM((n * G // 16, 16, ch), jnp.bfloat16) for _, _, G in PARTS]
    tiles = pltpu.VMEM((n, own, 8, n), jnp.bfloat16)
    wide = pltpu.VMEM((n * n // 16 * 4, 128), jnp.float32)
    half = pltpu.VMEM((own, n * rows // 2), jnp.bfloat16)
    small = pltpu.VMEM((layers, ch), jnp.float32)
    dma = pltpu.SemaphoreType.DMA
    got, second = pl.pallas_call(
        move_kernel,
        out_shape=[
            jax.ShapeDtypeStruct((n, own, 8, n), jnp.bfloat16),
            jax.ShapeDtypeStruct((own, n * rows // 2), jnp.bfloat16),
        ],
        in_specs=[hbm] * 7,
        out_specs=[hbm] * 2,
        scratch_shapes=states
        + [
            pltpu.VMEM((2, n // 2 + 2 * PAD, 16, ch), jnp.bfloat16),
            pltpu.VMEM((ch // 128, n * 8, 128), jnp.float32),
            pltpu.VMEM((ch * 8, 128), jnp.float32),
            pltpu.VMEM((2, n, own, 8, n), jnp.bfloat16),
            tiles,
            wide,
            half,
            pltpu.VMEM((layers, 3 * ch, ch), jnp.bfloat16),
            small,
            small,
            small,
            pltpu.VMEM((layers, ch, hid), jnp.bfloat16),
            pltpu.VMEM((layers, hid, ch), jnp.bfloat16),
            dma((6,)),
            dma((2,)),
            dma((3,)),
            dma((2,)),
            dma((2,)),
            dma,
        ],
        compiler_params=pltpu.CompilerParams(
            vmem_limit_bytes=VMEM, collective_id=0, has_side_effects=True
        ),
    )(activations, taps, conv_bias, conv_gain, mlp_gain, w_in, w_out)
    return pl.pallas_call(
        turn_kernel,
        out_shape=jax.ShapeDtypeStruct((own, n * rows), jnp.bfloat16),
        in_specs=[hbm] * 2,
        out_specs=hbm,
        scratch_shapes=[
            tiles,
            half,
            wide,
            pltpu.VMEM((own, n * rows), jnp.bfloat16),
            dma((8,)),
            dma,
            dma((4,)),
        ],
        compiler_params=pltpu.CompilerParams(vmem_limit_bytes=VMEM),
    )(got, second)


def solution(mesh):
    in_specs = (P("seq", None), P(), P(), P(), P(), P(), P())
    out_specs = P("seq", None)
    return jax.shard_map(shards, mesh=mesh, in_specs=in_specs, out_specs=out_specs, check_vma=False)
```

```python
import functools

import jax
import jax.numpy as jnp
from jax import lax
from jax.experimental import pallas as pl
from jax.experimental.pallas import tpu as pltpu
from jax.sharding import PartitionSpec as P

PAD = 8
PARTS = ((0, 0, 4), (1, 0, 8), (0, 4, 4))
VMEM = 63 * 1024 * 1024
MESH = pl.DeviceIdType.MESH


def gelu(x):
    half = 0.5 * x
    return half + half * lax.erf(x * 0.7071067811865476)


def rms(wide, gain):
    inverse = lax.rsqrt(jnp.mean(wide * wide, axis=-1, keepdims=True) + 1e-06)
    return (wide * inverse * gain).astype(jnp.bfloat16)


def tower(state, normed, flat, cw, cb, cg, mg, wi, wo, G):
    nb, _, ch = state.shape
    layers = cw.shape[0]
    rows = nb * 16

    def load():
        return state[...].reshape(rows, ch).astype(jnp.float32)

    def put(buf, wide, gain):
        normed[buf, pl.ds(PAD, nb)] = rms(wide, gain[None, :]).reshape(nb, 16, ch)
        tail = normed[buf, pl.ds(nb, PAD)].astype(jnp.float32)
        head = normed[buf, pl.ds(PAD, PAD)].astype(jnp.float32)
        zero = jnp.zeros((PAD, G, ch), jnp.float32)
        normed[buf, pl.ds(0, PAD)] = jnp.concatenate([zero, tail[:, : 16 - G]], axis=1).astype(jnp.bfloat16)
        normed[buf, pl.ds(PAD + nb, PAD)] = jnp.concatenate([head[:, G:], zero], axis=1).astype(jnp.bfloat16)

    def body(layer, last):
        cur = lax.rem(layer, 2)
        d = lax.shift_left(1, layer)
        lhs = jnp.concatenate([normed[cur, pl.ds(PAD + s, nb)].reshape(rows, ch) for s in (-d, 0, d)], axis=1)
        pre = jnp.dot(lhs, cw[layer], preferred_element_type=jnp.float32) + cb[layer, :][None, :]
        middle = (load() + gelu(pre)).astype(jnp.bfloat16)
        wide = middle.astype(jnp.float32)
        inner = rms(wide, mg[layer, :][None, :])
        hidden = gelu(jnp.dot(inner, wi[layer], preferred_element_type=jnp.float32)).astype(jnp.bfloat16)
        out = wide + jnp.dot(hidden, wo[layer], preferred_element_type=jnp.float32)
        if last:
            for j in range(ch // 128):
                flat[j, pl.ds(0, rows)] = out[:, j * 128 : (j + 1) * 128]
        else:
            new = out.astype(jnp.bfloat16)
            state[...] = new.reshape(nb, 16, ch)
            put(1 - cur, new.astype(jnp.float32), cg[layer + 1, :])

    def one_layer(layer, carry):
        body(layer, False)
        return carry

    put(0, load(), cg[0, :])
    lax.fori_loop(0, layers - 1, one_layer, 0)
    body(layers - 1, True)


def emit(part, flat, turned, packed, nb):
    pair, first, G = part
    for k in range(flat.shape[0]):
        for o in range(G):
            rows = [flat[k, pl.ds(f * G + o, nb, stride=16), :] for f in range(16 // G)]
            turned[pl.ds(k * 128 * G + o, 128, stride=G), :] = jnp.concatenate(rows, axis=0).T
    own, step = packed.shape[2], 64 // G

    def cast(g, carry):
        values = turned[pl.ds(pl.multiple_of(g * step * own * G, 8), step * own * G), :]
        packed[pair, pl.ds(g * step, step), :, pl.ds(first, G)] = values.astype(jnp.bfloat16).reshape(step, own, G, 128)
        return carry

    lax.fori_loop(0, packed.shape[1] // step, cast, 0)


def turn(got, wide, after=()):
    n, own, rows, _ = got.shape
    per = 128 // rows
    for b in range(n // per):
        if b < len(after):
            after[b].wait()
        for r in range(own):
            tile = got[pl.ds(b * per, per), r].reshape(128, n).astype(jnp.float32)
            wide[pl.ds(b * 4 + r, n, stride=4 * (n // per)), :] = tile.T


def turned_row(wide, i, blocks):
    base = pl.multiple_of(i * blocks * 4, 4)
    row = jnp.concatenate([wide[pl.ds(base + 4 * b, 4), :] for b in range(blocks)], axis=1)
    return row[:3].astype(jnp.bfloat16)


def move_kernel(
    x_hbm, cw_hbm, cb_hbm, cg_hbm, mg_hbm, wi_hbm, wo_hbm, got, half_hbm,
    state_a, state_b, state_c, normed, flat, turned, packed, got_b, wide, half, cw, cb, cg, mg, wi, wo,
    load_sem, in_send, in_recv, out_send, out_recv, half_sem,
):
    me = lax.axis_index("seq")
    n = packed.shape[1]
    states = state_a, state_b, state_c
    loads = [
        pltpu.make_async_copy(s, d, load_sem.at[k])
        for k, (s, d) in enumerate(
            ((cw_hbm, cw), (cb_hbm, cb), (cg_hbm, cg), (mg_hbm, mg), (wi_hbm, wi), (wo_hbm, wo))
        )
    ]
    for load in loads:
        load.start()

    xs = [lax.rem(me // 32 + k, 4) * 32 for k in range(4)]
    cores = [lax.rem(me + k, 2) for k in range(2)]
    ends = [x + core for x in xs for core in cores]
    z_me, y_me = lax.rem(me // 8, 4), lax.rem(me // 2, 4)

    def each_peer(act):
        for end in ends[1:]:
            act(end + z_me * 8 + y_me * 2)

        def step(g, carry):
            y = lax.rem(g, 4)
            z = lax.rem(g // 4 + y, 4)
            middle = lax.rem(z_me + z, 4) * 8 + lax.rem(y_me + y, 4) * 2
            for end in ends:
                act(end + middle)
            return carry

        lax.fori_loop(1, n // len(ends), step, 0)

    zs = [lax.rem(z_me + k, 4) * 8 for k in range(4)]
    ys = [lax.rem(y_me + k, 4) * 2 for k in range(4)]
    hops = (0, 1, 2, 1)
    steps = [(x, y, z, c) for y in range(4) for z in range(4) for x in range(4) for c in range(2)][1:]
    steps.sort(key=lambda s: -hops[s[0]] - hops[s[1]] - hops[s[2]])
    middles = {(y, z): ys[y] + zs[z] for y in range(4) for z in range(4)}

    def far_first(act):
        for x, y, z, c in steps:
            act(ends[x * 2 + c] + middles[y, z])

    barrier = pltpu.get_barrier_semaphore()
    each_peer(lambda j: pl.semaphore_signal(barrier, inc=1, device_id=(j,), device_id_type=MESH))
    pl.semaphore_wait(barrier, n - 1)

    for k, (pair, first, G) in enumerate(PARTS):
        nb = states[k].shape[0]
        place = states[k].at[lax.rem(me, nb), pl.ds(me // nb * G, G)]

        def source(j):
            return x_hbm.at[pl.ds((pair * n + j) * 8 + first, G)]

        pltpu.make_async_copy(source(me), place, in_recv.at[k]).start()
        (far_first if k == 0 else each_peer)(
            lambda j: pltpu.make_async_remote_copy(
                source(j), place, in_send.at[pair], in_recv.at[k], device_id=(j,), device_id_type=MESH
            ).start()
        )
    for load in loads:
        load.wait()

    for k, part in enumerate(PARTS):
        pair, first, G = part
        state = states[k]
        pltpu.make_async_copy(state, state, in_recv.at[k]).wait()
        tower(state, normed, flat, cw, cb, cg, mg, wi, wo, G)
        emit(part, flat, turned, packed, state.shape[0])
        rows = pl.ds(first, G)
        place = (got_b if pair else got).at[me, :, rows]
        pltpu.make_async_copy(packed.at[pair, me, :, rows], place, out_recv.at[pair]).start()
        (far_first if k == len(PARTS) - 1 else each_peer)(
            lambda j: pltpu.make_async_remote_copy(
                packed.at[pair, j, :, rows], place, out_send.at[pair], out_recv.at[pair],
                device_id=(j,), device_id_type=MESH,
            ).start()
        )

    pltpu.make_async_copy(got_b, got_b, out_recv.at[1]).wait()
    turn(got_b, wide)
    blocks = n // 16
    width = blocks * 128

    def store(g, carry):
        for k in range(4):
            i = g * 4 + k
            half[:, pl.ds(pl.multiple_of(i * width, 128), width)] = turned_row(wide, i, blocks)
        return carry

    lax.fori_loop(0, n // 4, store, 0)
    out = pltpu.make_async_copy(half, half_hbm, half_sem)
    out.start()
    for pair in range(2):
        sent = x_hbm.at[pl.ds(0, (n - 1) * 8)]
        pltpu.make_async_copy(sent, sent, in_send.at[pair]).wait()
        sent = packed.at[pair, pl.ds(0, n - 1)]
        pltpu.make_async_copy(sent, sent, out_send.at[pair]).wait()
    out.wait()
    pltpu.make_async_copy(got, got, out_recv.at[0]).wait()


def turn_kernel(got_hbm, half_hbm, out_hbm, got, half, wide, out, load_sem, half_sem, out_sem):
    n = got.shape[0]
    quarter = n // 4
    loads = []
    for b in range(8):
        part = pl.ds(b * 16, 16)
        loads.append(pltpu.make_async_copy(got_hbm.at[part], got.at[part], load_sem.at[b]))
        loads[-1].start()
    other = pltpu.make_async_copy(half_hbm, half, half_sem)
    other.start()
    turn(got, wide, loads)
    other.wait()
    blocks = n // 16
    width = blocks * 128
    stores = []
    for h in range(4):
        def store(g, carry):
            for k in range(4):
                i = h * quarter + g * 4 + k
                base = pl.multiple_of(i * 2 * width, 128)
                out[:, pl.ds(base, width)] = turned_row(wide, i, blocks)
                out[:, pl.ds(base + width, width)] = half[:, pl.ds(pl.multiple_of(i * width, 128), width)]
            return carry

        lax.fori_loop(0, quarter // 4, store, 0)
        part = slice(None), pl.ds(h * quarter * 2 * width, quarter * 2 * width)
        stores.append(pltpu.make_async_copy(out.at[part], out_hbm.at[part], out_sem.at[h]))
        stores[-1].start()
    for copy in stores:
        copy.wait()


def shards(activations, conv_weight, conv_bias, conv_gain, mlp_gain, w_in, w_out):
    n = lax.axis_size("seq")
    rows, ch = activations.shape
    layers = conv_weight.shape[0]
    hid = w_in.shape[2]
    own = ch // n
    taps = conv_weight.reshape(layers, 3 * ch, ch)
    hbm = pl.BlockSpec(memory_space=pl.ANY)
    states = [pltpu.VMEM((n * G // 16, 16, ch), jnp.bfloat16) for _, _, G in PARTS]
    tiles = pltpu.VMEM((n, own, 8, n), jnp.bfloat16)
    wide = pltpu.VMEM((n * n // 16 * 4, 128), jnp.float32)
    half = pltpu.VMEM((own, n * rows // 2), jnp.bfloat16)
    small = pltpu.VMEM((layers, ch), jnp.float32)
    dma = pltpu.SemaphoreType.DMA
    got, second = pl.pallas_call(
        move_kernel,
        out_shape=[
            jax.ShapeDtypeStruct((n, own, 8, n), jnp.bfloat16),
            jax.ShapeDtypeStruct((own, n * rows // 2), jnp.bfloat16),
        ],
        in_specs=[hbm] * 7,
        out_specs=[hbm] * 2,
        scratch_shapes=states
        + [
            pltpu.VMEM((2, n // 2 + 2 * PAD, 16, ch), jnp.bfloat16),
            pltpu.VMEM((ch // 128, n * 8, 128), jnp.float32),
            pltpu.VMEM((ch * 8, 128), jnp.float32),
            pltpu.VMEM((2, n, own, 8, n), jnp.bfloat16),
            tiles,
            wide,
            half,
            pltpu.VMEM((layers, 3 * ch, ch), jnp.bfloat16),
            small,
            small,
            small,
            pltpu.VMEM((layers, ch, hid), jnp.bfloat16),
            pltpu.VMEM((layers, hid, ch), jnp.bfloat16),
            dma((6,)),
            dma((2,)),
            dma((3,)),
            dma((2,)),
            dma((2,)),
            dma,
        ],
        compiler_params=pltpu.CompilerParams(
            vmem_limit_bytes=VMEM, collective_id=0, has_side_effects=True
        ),
    )(activations, taps, conv_bias, conv_gain, mlp_gain, w_in, w_out)
    return pl.pallas_call(
        turn_kernel,
        out_shape=jax.ShapeDtypeStruct((own, n * rows), jnp.bfloat16),
        in_specs=[hbm] * 2,
        out_specs=hbm,
        scratch_shapes=[
            tiles,
            half,
            wide,
            pltpu.VMEM((own, n * rows), jnp.bfloat16),
            dma((8,)),
            dma,
            dma((4,)),
        ],
        compiler_params=pltpu.CompilerParams(vmem_limit_bytes=VMEM),
    )(got, second)


def solution(mesh):
    in_specs = (P("seq", None), P(), P(), P(), P(), P(), P())
    out_specs = P("seq", None)
    return jax.shard_map(shards, mesh=mesh, in_specs=in_specs, out_specs=out_specs, check_vma=False)
```
